32 devices in a mesh: head: 4 (over z), ctx: 8 (over y, x, core).
Axes of the slice: x: 2, y: 2, z: 4, core: 2. Of those that a mesh axis runs over, the one named last changes fastest.
Arguments:
- queries: bfloat16 [8, 256, 4096], P('ctx', 'head'), may hold values from -6 to 6
- key_state_rows: bfloat16 [8, 256, 512], P('ctx', 'head'), may hold values from -6 to 6
- value_state_rows: bfloat16 [8, 256, 512], P('ctx', 'head'), may hold values from -6 to 6
- output_state_rows: bfloat16 [8, 256, 4096], P('ctx', 'head'), may hold values from -6 to 6
- output_gradient: bfloat16 [8, 256, 4096], P('ctx', 'head'), may hold values from -0.5390625 to 0.5390625
- logsumexp_rows: float32 [8, 256, 32], P('ctx', None, 'head'), may hold values from 2 to 4
- doc_lengths: int32 [8], replicated, may hold values from 1 to 1024, 2048 in all
Outputs:
- query_grad: bfloat16 [8, 256, 4096], P('ctx', 'head')
- gradient_keys: bfloat16 [8, 256, 512], P('ctx', 'head')
- gradient_values: bfloat16 [8, 256, 512], P('ctx', 'head')
The draws below stay inside these ranges and needn't reach their ends.
Inputs may be any that keep to these rules, and one draw needn't show every extreme that they name: `doc_lengths`: the 8 lengths sum to 2048; the longest is exactly 1024.
All inputs are finite; a program needn't handle non-finite values.
Results may differ from the reference program's by a relative error of at most 0.0049.
Values may be sent and summed in bfloat16 or wider, within the bound.
No kernel may reach another device: no remote copies, remote signals or barrier semaphores. Data moves between devices by JAX's collectives and lax.ppermute only.
A program may use at most 64 MiB of HBM per device.

```python
import math
import jax
import jax.numpy as jnp
import numpy as np
from jax import lax

QUERY_HEAD_COUNT = 32
KEY_VALUE_HEADS = 4
HEAD_WIDTH = 128
LAGS = 4
CONTEXT_TOKENS = 256
TOKENS = 2048
MAXDOC = 1024
DOCS = 8
N_CTX = 8


def shard_levels(rng, shape, shards, least, largest):
    def one(dim, parts):
        heights = jax.random.uniform(jax.random.fold_in(jax.random.fold_in(rng, 6), dim), (parts,), jnp.float32, least / len(shards), largest / len(shards))
        return jnp.repeat(jnp.exp(heights), shape[dim] // parts).reshape((-1,) + (1,) * (len(shape) - dim - 1))

    gain = one(*shards[0])
    for cut in shards[1:]:
        gain = gain * one(*cut)
    return gain


def length_profile(number_of, total, bound, skew):
    weights = [(1 << 20) // math.isqrt(standing ** skew) + 1 for standing in range(2, number_of + 1)]
    spare, holding = total - bound - (number_of - 1), [1] * (number_of - 1)
    while spare > 0:
        movable = [i for i in range(number_of - 1) if holding[i] < bound]
        whole, budget = sum([weights[i] for i in movable]), spare
        for i in movable:
            addition = min(bound - holding[i], max(1, budget * weights[i] // whole), spare)
            holding[i] = holding[i] + addition
            spare = spare - addition
    return np.array([bound] + holding)


def uneven_parts(key, number_of, total, reach, lean):
    if number_of == 2:
        one = jax.random.randint(key, (), max(1, total - reach), min(reach, total - 1) + 1)
        return jnp.stack([one, total - one])
    lengths = jnp.asarray(length_profile(number_of, total, reach, lean), jnp.int32)
    couples = (number_of - 1) // 2
    giver, receiver = lengths[1:1 + 2 * couples:2], lengths[2:2 + 2 * couples:2]
    room = jnp.minimum(giver - 1, reach - receiver)
    passed = jax.random.randint(jax.random.fold_in(key, 1), (couples,), 0, 1 << 20) % (room + 1)
    lengths = lengths.at[1:1 + 2 * couples:2].set(giver - passed).at[2:2 + 2 * couples:2].set(receiver + passed)
    return lengths[jax.random.permutation(jax.random.fold_in(key, 2), number_of)]


def centred(own_key, extent, scale, bound, cuts=(), held_as=jnp.bfloat16):
    entries = jax.random.normal(own_key, extent, jnp.float32) * scale
    if len(cuts) > 0:
        entries = shard_levels(own_key, extent, cuts, -0.22, 0.18) * entries
    return jnp.clip(entries, min=-bound, max=bound).astype(held_as)


def setup_inputs(seed: int = 0) -> dict:
    seeds = jax.random.split(jax.random.key(seed), 8)
    return {
        "queries": centred(seeds[0], (N_CTX, CONTEXT_TOKENS, QUERY_HEAD_COUNT * HEAD_WIDTH), 1.0, 6.0, ((0, 8), (1, 4))),
        "key_state_rows": centred(seeds[1], (N_CTX, CONTEXT_TOKENS, KEY_VALUE_HEADS * HEAD_WIDTH), 1.0, 6.0, ((0, 8), (1, 4))),
        "value_state_rows": centred(seeds[2], (N_CTX, CONTEXT_TOKENS, KEY_VALUE_HEADS * HEAD_WIDTH), 1.0, 6.0, ((0, 8), (1, 4))),
        "output_state_rows": centred(seeds[3], (N_CTX, CONTEXT_TOKENS, QUERY_HEAD_COUNT * HEAD_WIDTH), 1.0, 6.0, ((0, 8), (1, 4))),
        "output_gradient": centred(seeds[4], (N_CTX, CONTEXT_TOKENS, QUERY_HEAD_COUNT * HEAD_WIDTH), 0.09, 0.5390625, ((0, 8), (1, 4))),
        "logsumexp_rows": jnp.clip(2.0 + 2.0 * jax.random.uniform(seeds[5], (N_CTX, CONTEXT_TOKENS, QUERY_HEAD_COUNT), jnp.float32) ** shard_levels(seeds[5], (N_CTX, CONTEXT_TOKENS, QUERY_HEAD_COUNT), ((0, 8), (2, 4)), -0.2, 0.2), 2.0, 4.0),
        "doc_lengths": uneven_parts(seeds[6], DOCS, TOKENS, MAXDOC, 2).astype(jnp.int32),
    }


def segment_of(positions, starts):
    return jnp.sum((starts[None, :] <= positions[:, None]).astype(jnp.int32), axis=1) - 1


def block_terms(query_block, grad_block, sums_turned, delta_turned, key_block, value_block, allowed):
    score_scale = HEAD_WIDTH ** -0.5
    query_wide = query_block.astype(jnp.float32)
    grad_wide = grad_block.astype(jnp.float32)
    key_wide = key_block.astype(jnp.float32)
    value_wide = value_block.astype(jnp.float32)
    scores = jnp.einsum("ikgd,jkd->kgij", query_wide, key_wide) * score_scale
    weights = jnp.where(allowed[None, None], jnp.exp(scores - sums_turned), 0.0)
    grad_scores = jnp.einsum("ikgd,jkd->kgij", grad_wide, value_wide)
    shifted = (weights * (grad_scores - delta_turned) * score_scale).astype(jnp.bfloat16)
    rounded = weights.astype(jnp.bfloat16)
    value_part = jnp.einsum("kgij,ikgd->jkd", rounded.astype(jnp.float32), grad_wide)
    key_part = jnp.einsum("kgij,ikgd->jkd", shifted.astype(jnp.float32), query_wide)
    query_part = jnp.einsum("kgij,jkd->ikgd", shifted.astype(jnp.float32), key_wide)
    return query_part, key_part, value_part


def reference(queries, key_state_rows, value_state_rows, output_state_rows, output_gradient, logsumexp_rows, doc_lengths):
    block_list = N_CTX
    row_list = CONTEXT_TOKENS
    group_count = QUERY_HEAD_COUNT // KEY_VALUE_HEADS
    starts = (jnp.cumsum(doc_lengths) - doc_lengths).astype(jnp.int32)
    query_every = queries.reshape(block_list, row_list, KEY_VALUE_HEADS, group_count, HEAD_WIDTH)
    gradient_every = output_gradient.reshape(block_list, row_list, KEY_VALUE_HEADS, group_count, HEAD_WIDTH)
    output_every = output_state_rows.reshape(block_list, row_list, KEY_VALUE_HEADS, group_count, HEAD_WIDTH)
    key_every = key_state_rows.reshape(block_list, row_list, KEY_VALUE_HEADS, HEAD_WIDTH)
    value_every = value_state_rows.reshape(block_list, row_list, KEY_VALUE_HEADS, HEAD_WIDTH)
    delta_all = jnp.sum(gradient_every.astype(jnp.float32) * output_every.astype(jnp.float32), axis=-1)
    sum_every = logsumexp_rows.reshape(block_list, row_list, KEY_VALUE_HEADS, group_count)
    offsets = jnp.arange(row_list, dtype=jnp.int32)
    blank_terms = (jnp.zeros((row_list, KEY_VALUE_HEADS, group_count, HEAD_WIDTH), jnp.float32),
                   jnp.zeros((row_list, KEY_VALUE_HEADS, HEAD_WIDTH), jnp.float32),
                   jnp.zeros((row_list, KEY_VALUE_HEADS, HEAD_WIDTH), jnp.float32))

    def step(carry, block_index):
        key_gradient_list, value_gradient_list = carry
        query_pos = block_index * row_list + offsets
        query_seg = segment_of(query_pos, starts)
        query_block = query_every[block_index]
        grad_block = gradient_every[block_index]
        sums_turned = jnp.transpose(sum_every[block_index], (1, 2, 0))[..., None]
        delta_turned = jnp.transpose(delta_all[block_index], (1, 2, 0))[..., None]
        query_overall = jnp.zeros((row_list, KEY_VALUE_HEADS, group_count, HEAD_WIDTH), jnp.float32)
        for distance in range(LAGS + 1):
            source = jnp.maximum(block_index - distance, 0).astype(jnp.int32)
            key_pos = (block_index - distance) * row_list + offsets
            key_seg = segment_of(key_pos, starts)
            allowed = ((query_seg[:, None] == key_seg[None, :])
                       & (key_pos[None, :] <= query_pos[:, None])
                       & (key_pos[None, :] >= 0))
            key_block = key_every[source]
            value_block = value_every[source]
            query_part, key_part, value_part = lax.cond(
                jnp.any(allowed),
                lambda: block_terms(query_block, grad_block, sums_turned, delta_turned,
                                    key_block, value_block, allowed),
                lambda: blank_terms)
            query_overall = query_overall + query_part
            key_gradient_list = key_gradient_list.at[source].add(key_part)
            value_gradient_list = value_gradient_list.at[source].add(value_part)
        return (key_gradient_list, value_gradient_list), query_overall

    initial_carry = (jnp.zeros((block_list, row_list, KEY_VALUE_HEADS, HEAD_WIDTH), jnp.float32),
                   jnp.zeros((block_list, row_list, KEY_VALUE_HEADS, HEAD_WIDTH), jnp.float32))
    (key_gradient_list, value_gradient_list), query_grads = lax.scan(step, initial_carry, jnp.arange(block_list, dtype=jnp.int32))
    query_grad = query_grads.reshape(block_list, row_list, QUERY_HEAD_COUNT * HEAD_WIDTH).astype(jnp.bfloat16)
    gradient_keys = key_gradient_list.reshape(block_list, row_list, KEY_VALUE_HEADS * HEAD_WIDTH).astype(jnp.bfloat16)
    gradient_values = value_gradient_list.reshape(block_list, row_list, KEY_VALUE_HEADS * HEAD_WIDTH).astype(jnp.bfloat16)
    return query_grad, gradient_keys, gradient_values
```

```python
import functools

import jax
import jax.numpy as jnp
from jax import lax
from jax.experimental import pallas as pl
from jax.experimental.pallas import tpu as pltpu
from jax.sharding import PartitionSpec as P

QUERY_HEAD_COUNT = 32
KEY_VALUE_HEADS = 4
GROUP = QUERY_HEAD_COUNT // KEY_VALUE_HEADS
D = 128
LAGS = 4
TILE = 256
BF = jnp.bfloat16
F32 = jnp.float32
NT = (((1,), (1,)), ((), ()))
NN = (((1,), (0,)), ((), ()))
TN = (((0,), (0,)), ((), ()))


def lanes(start, size):
    return pl.ds(pl.multiple_of(start, size), size)


def vmem_specs(count):
    return [pl.BlockSpec(memory_space=pltpu.VMEM)] * count


def cost(flops, nbytes):
    return pl.CostEstimate(flops=flops, bytes_accessed=nbytes, transcendentals=0)


def three_way(x):
    hi = x.astype(BF)
    rest = x - hi.astype(F32)
    mid = rest.astype(BF)
    low = (rest - mid.astype(F32)).astype(BF)
    return hi, mid, low


def pack_kv_body(heads, k_ref, v_ref, *outs):
    me = lax.axis_index("head")
    for s in range(1, heads):
        to = me ^ s
        outs[s - 1][:, :D] = k_ref[:, lanes(to * D, D)]
        outs[s - 1][:, D:] = v_ref[:, lanes(to * D, D)]


def pack_qdo_body(heads, q_ref, g_ref, o_ref, *outs):
    me = lax.axis_index("head")
    rows = q_ref.shape[0]
    width = GROUP * D
    lane = lax.broadcasted_iota(jnp.int32, (rows, D), 1)
    for s in range(heads):
        to = me ^ s
        out = outs[s]
        out[:, :width] = q_ref[:, lanes(to * width, width)]
        grad = g_ref[:, lanes(to * width, width)]
        out[:, width : 2 * width] = grad
        prod = grad.astype(F32) * o_ref[:, lanes(to * width, width)].astype(F32)
        delta = jnp.zeros((rows, D), F32)
        for h in range(GROUP):
            one = jnp.sum(prod[:, h * D : (h + 1) * D], axis=1, keepdims=True)
            delta = jnp.where(lane % GROUP == h, one, delta)
        hi, mid, low = three_way(delta)
        part = lane // GROUP
        zero = jnp.zeros_like(hi)
        out[:, 2 * width :] = jnp.where(
            part == 0, hi, jnp.where(part == 1, mid, jnp.where(part == 2, low, zero))
        )


def assemble_body(heads, k_ref, v_ref, *refs):
    me = lax.axis_index("head")
    out = refs[-1]
    rows = k_ref.shape[0]
    out[lanes(me * rows, rows), :D] = k_ref[:, lanes(me * D, D)]
    out[lanes(me * rows, rows), D:] = v_ref[:, lanes(me * D, D)]
    for s in range(1, heads):
        out[lanes((me ^ s) * rows, rows), :] = refs[s - 1][...]


def compute_body(shifts, first, last, block, lens_ref, lse_ref, *refs):
    me = lax.axis_index("head")
    ctx = lax.axis_index("ctx")
    refs = list(refs)
    kv_refs = refs[: LAGS + 1]
    refs = refs[LAGS + 1 :]
    chunk_refs = refs[: len(shifts)]
    refs = refs[len(shifts) :]
    acc_in = None
    if not first:
        acc_in = refs.pop(0)
    dq_refs = refs[: len(shifts)]
    refs = refs[len(shifts) :]
    if last:
        back_refs = refs[: LAGS + 1]
        refs = refs[LAGS + 1 :]
    else:
        acc_out = refs.pop(0)
    kv, acc, qa, ga, dqt = refs

    rows = chunk_refs[0].shape[0]
    width = GROUP * D
    total = (LAGS + 1) * block
    scale = float(D) ** (-0.5)
    log2e = 1.4426950408889634

    for lag in range(LAGS + 1):
        at = (LAGS - lag) * block
        kv[at : at + block, :] = kv_refs[lag][...]
    if first:
        acc[...] = jnp.zeros_like(acc)
    else:
        acc[...] = acc_in[...]

    base = (ctx - LAGS) * block
    lane = lax.broadcasted_iota(jnp.int32, (rows, D), 1)
    part = lane // GROUP
    minus = jnp.where(
        lax.broadcasted_iota(jnp.int32, (TILE, D), 1) < 3 * GROUP, -1.0, 0.0
    ).astype(BF)
    key_iota = lax.broadcasted_iota(jnp.int32, (TILE, D), 0)
    token = lax.broadcasted_iota(jnp.int32, (1, D), 1) % rows

    for n, s in enumerate(shifts):
        src = me ^ s
        chunk = chunk_refs[n]
        first_pos = ctx * block + src * rows
        pos = first_pos + token
        low_first = jnp.int32(0)
        low = jnp.zeros_like(pos)
        begin = jnp.int32(0)
        for d in range(lens_ref.shape[0]):
            low_first = jnp.where(begin <= first_pos, begin, low_first)
            low = jnp.where(begin <= pos, begin, low)
            begin = begin + lens_ref[d]
        low = low - base
        high = pos - base
        lse = lse_ref[lanes(src * rows, rows), :] * (1.0 / scale)
        wide = jnp.zeros((rows, D), F32)
        for h in range(GROUP):
            wide = jnp.where(lane % GROUP == h, lse[:, h : h + 1], wide)
        hi, mid, lo3 = three_way(wide)
        zero = jnp.zeros_like(hi)
        lse3 = jnp.where(part == 0, hi, jnp.where(part == 1, mid, jnp.where(part == 2, lo3, zero)))
        del3 = chunk[:, 2 * width :]
        for h in range(GROUP):
            mine = lane % GROUP == h
            at = h * rows
            qa[at : at + rows, :D] = chunk[:, h * D : (h + 1) * D]
            qa[at : at + rows, D:] = jnp.where(mine, lse3, zero)
            ga[at : at + rows, :D] = chunk[:, width + h * D : width + (h + 1) * D]
            ga[at : at + rows, D:] = jnp.where(mine, del3, zero)
        dqt[...] = jnp.zeros_like(dqt)

        def tile_step(t, carry):
            at = pl.multiple_of(t * TILE, TILE)
            k_tile = kv[pl.ds(at, TILE), :D]
            v_tile = kv[pl.ds(at, TILE), D:]
            ka = jnp.concatenate([k_tile, minus], axis=1)
            va = jnp.concatenate([v_tile, minus], axis=1)
            key = key_iota + at
            ok = (key >= low) & (key <= high)
            okw = jnp.concatenate([ok] * (GROUP * rows // D), axis=1)
            st = lax.dot_general(ka, qa[...], NT, preferred_element_type=F32)
            w = jnp.where(okw, jnp.exp2(st * (scale * log2e)), 0.0)
            dp = lax.dot_general(va, ga[...], NT, preferred_element_type=F32)
            ds = (w * dp * scale).astype(BF)
            wb = w.astype(BF)
            acc[pl.ds(at, TILE), D:] += lax.dot_general(
                wb, ga[:, :D], NN, preferred_element_type=F32
            )
            acc[pl.ds(at, TILE), :D] += lax.dot_general(
                ds, qa[:, :D], NN, preferred_element_type=F32
            )
            dqt[...] += lax.dot_general(k_tile, ds, TN, preferred_element_type=F32)
            return carry

        t_lo = jnp.maximum(low_first - base, 0) // TILE
        t_hi = (first_pos + rows - 1 - base) // TILE
        lax.fori_loop(t_lo, t_hi + 1, tile_step, 0)
        dq = jnp.transpose(dqt[...])
        for h in range(GROUP):
            dq_refs[n][:, h * D : (h + 1) * D] = dq[h * rows : (h + 1) * rows, :].astype(BF)

    if last:
        for lag in range(LAGS + 1):
            at = (LAGS - lag) * block
            back_refs[lag][...] = acc[at : at + block, :].astype(back_refs[lag].dtype)
    else:
        acc_out[...] = acc[...]


def sum_body(heads, own_ref, *refs):
    me = lax.axis_index("head")
    parts = refs[:LAGS]
    outs = refs[LAGS:]
    rows = outs[0].shape[0]
    for s in range(heads):
        at = lanes((me ^ s) * rows, rows)
        total = own_ref[at, :]
        for part in parts:
            total = total + part[at, :].astype(F32)
        outs[s][...] = total.astype(BF)


def finish_q_body(heads, *refs):
    me = lax.axis_index("head")
    out = refs[-1]
    width = GROUP * D
    for s in range(heads):
        out[:, lanes((me ^ s) * width, width)] = refs[s][...]


def finish_kv_body(heads, *refs):
    me = lax.axis_index("head")
    dk, dv = refs[-2:]
    for s in range(heads):
        dk[:, lanes((me ^ s) * D, D)] = refs[s][:, :D]
        dv[:, lanes((me ^ s) * D, D)] = refs[s][:, D:]


def swap(x, s):
    n = lax.axis_size("head")
    return lax.ppermute(x, "head", [(i, i ^ s) for i in range(n)])


def along(x, distance):
    n = lax.axis_size("ctx")
    return lax.ppermute(x, "ctx", [(i - distance, i) for i in range(n) if 0 <= i - distance < n])


def shape(*dims, dtype=BF):
    return jax.ShapeDtypeStruct(dims, dtype)


def call(body, outs, args, flops=0, scratch=(), smem=0):
    nbytes = sum(a.size * a.dtype.itemsize for a in list(args) + list(outs))
    return pl.pallas_call(
        body,
        out_shape=list(outs),
        in_specs=[pl.BlockSpec(memory_space=pltpu.SMEM)] * smem + vmem_specs(len(args) - smem),
        out_specs=vmem_specs(len(outs)),
        scratch_shapes=list(scratch),
        cost_estimate=cost(flops, nbytes),
    )(*args)


def local(queries, key_rows, value_rows, output_rows, output_grad, lse_rows, doc_lengths):
    rows = queries.shape[1]
    heads = lax.axis_size("head")
    block = rows * heads
    width = GROUP * D
    q, k, v, o, g = (x[0] for x in (queries, key_rows, value_rows, output_rows, output_grad))
    lse = lse_rows[0]

    kv_out = call(
        functools.partial(pack_kv_body, heads), [shape(rows, 2 * D)] * (heads - 1), [k, v]
    )
    kv_in = [swap(kv_out[s - 1], s) for s in range(1, heads)]
    qdo_out = call(
        functools.partial(pack_qdo_body, heads), [shape(rows, 2 * width + D)] * heads, [q, g, o]
    )
    chunks = [qdo_out[0]] + [swap(qdo_out[s], s) for s in range(1, heads)]
    (kv_own,) = call(
        functools.partial(assemble_body, heads), [shape(block, 2 * D)], [k, v] + kv_in
    )
    kv_blocks = [kv_own] + [along(kv_own, lag) for lag in range(1, LAGS + 1)]

    total = (LAGS + 1) * block
    scratch = [
        pltpu.VMEM((total, 2 * D), BF),
        pltpu.VMEM((total, 2 * D), F32),
        pltpu.VMEM((GROUP * rows, 2 * D), BF),
        pltpu.VMEM((GROUP * rows, 2 * D), BF),
        pltpu.VMEM((D, GROUP * rows), F32),
    ]
    plan = [[0, 1], [2], [3]]
    acc = None
    dq = {}
    for n, shifts in enumerate(plan):
        first, last = n == 0, n == len(plan) - 1
        outs = [shape(rows, width)] * len(shifts)
        if last:
            outs += [shape(block, 2 * D, dtype=F32)] + [shape(block, 2 * D)] * LAGS
        else:
            outs += [shape(total, 2 * D, dtype=F32)]
        args = [doc_lengths, lse] + kv_blocks + [chunks[s] for s in shifts]
        if not first:
            args.append(acc)
        res = call(
            functools.partial(compute_body, shifts, first, last, block),
            outs,
            args,
            flops=len(shifts) * 10 * total * rows * GROUP * D // 2,
            scratch=scratch,
            smem=1,
        )
        for i, s in enumerate(shifts):
            dq[s] = res[i]
        rest = res[len(shifts) :]
        if not last:
            acc = rest[0]
    own, backs = rest[0], rest[1:]
    parts = [along(backs[lag - 1], -lag) for lag in range(1, LAGS + 1)]
    dq_in = [dq[0]] + [swap(dq[s], s) for s in range(1, heads)]
    sums = call(
        functools.partial(sum_body, heads), [shape(rows, 2 * D)] * heads, [own] + parts
    )
    (query_grad,) = call(
        functools.partial(finish_q_body, heads), [shape(rows, heads * width)], dq_in
    )
    kv_grad = [sums[0]] + [swap(sums[s], s) for s in range(1, heads)]
    dk, dv = call(
        functools.partial(finish_kv_body, heads), [shape(rows, heads * D)] * 2, kv_grad
    )
    return query_grad[None], dk[None], dv[None]


def solution(mesh):
    in_specs = (
        P("ctx", "head", None),
        P("ctx", "head", None),
        P("ctx", "head", None),
        P("ctx", "head", None),
        P("ctx", "head", None),
        P("ctx", None, "head"),
        P(),
    )
    out_specs = (P("ctx", "head", None), P("ctx", "head", None), P("ctx", "head", None))
    return jax.shard_map(local, mesh=mesh, in_specs=in_specs, out_specs=out_specs, check_vma=False)
```

```python
import functools

import jax
import jax.numpy as jnp
from jax import lax
from jax.experimental import pallas as pl
from jax.experimental.pallas import tpu as pltpu
from jax.sharding import PartitionSpec as P


QUERY_HEAD_COUNT = 32
KEY_VALUE_HEADS = 4
GROUP = QUERY_HEAD_COUNT // KEY_VALUE_HEADS
D = 128
LAGS = 4
TILE = 256
PACK_LIMIT = 55000000
BF = jnp.bfloat16
F32 = jnp.float32
NT = (((1,), (1,)), ((), ()))
NN = (((1,), (0,)), ((), ()))
TN = (((0,), (0,)), ((), ()))


def lanes(start, size):
    return pl.ds(pl.multiple_of(start, size), size)


def vmem_specs(count):
    return [pl.BlockSpec(memory_space=pltpu.VMEM)] * count


def cost(flops, nbytes):
    return pl.CostEstimate(flops=flops, bytes_accessed=nbytes, transcendentals=0)


def three_way(x):
    hi = x.astype(BF)
    rest = x - hi.astype(F32)
    mid = rest.astype(BF)
    low = (rest - mid.astype(F32)).astype(BF)
    return hi, mid, low


def pack_kv_body(heads, k_ref, v_ref, *outs):
    me = lax.axis_index("head")
    for s in range(heads):
        at = lanes((me ^ s) * D, D)
        outs[s][:, :D] = k_ref[0, :, at]
        outs[s][:, D:] = v_ref[0, :, at]


def pack_body(heads, q_ref, g_ref, o_ref, *refs):
    q_ref, g_ref, o_ref = (ref.at[0] for ref in (q_ref, g_ref, o_ref))
    qdo_outs, (o_buf, sem) = refs[:heads], refs[heads:]
    me = lax.axis_index("head")
    rows = q_ref.shape[0]
    width = GROUP * D
    early, late = [], []
    for s in range(1, heads + 1):
        to = me ^ (s % heads)
        out = qdo_outs[s % heads]
        cols = lanes(to * width, width)
        early += [
            (g_ref.at[:, cols], out.at[:, width : 2 * width]),
            (o_ref.at[:, cols], o_buf.at[s % heads]),
        ]
        late += [(q_ref.at[:, cols], out.at[:, :width])]
    copies = [
        pltpu.make_async_copy(src, dst, sem.at[n]) for n, (src, dst) in enumerate(early + late)
    ]
    for copy in copies:
        copy.start()
    lane = lax.broadcasted_iota(jnp.int32, (rows, D), 1)
    part = lane // GROUP
    for n in range(heads):
        s = (n + 1) % heads
        copies[2 * n].wait()
        copies[2 * n + 1].wait()
        out = qdo_outs[s]
        prod = out[:, width : 2 * width].astype(F32) * o_buf[s].astype(F32)
        delta = jnp.zeros((rows, D), F32)
        for h in range(GROUP):
            one = jnp.sum(prod[:, h * D : (h + 1) * D], axis=1, keepdims=True)
            delta = jnp.where(lane % GROUP == h, one, delta)
        hi, mid, low = three_way(delta)
        zero = jnp.zeros_like(hi)
        out[:, 2 * width :] = jnp.where(
            part == 0, hi, jnp.where(part == 1, mid, jnp.where(part == 2, low, zero))
        )
    for copy in copies[len(early) :]:
        copy.wait()


def assemble_body(heads, *refs):
    me = lax.axis_index("head")
    out = refs[-1]
    rows = refs[0].shape[0]
    for s in range(heads):
        out[lanes((me ^ s) * rows, rows), :] = refs[s][...]


def compute_body(shifts, first, last, block, lens_ref, lse_ref, *refs):
    me = lax.axis_index("head")
    ctx = lax.axis_index("ctx")
    refs = list(refs)
    many = len(shifts)
    if first:
        own_ref, two_ref, four_ref, p_own_ref, p_two_ref, p_four_ref = refs[:6]
        chunk_refs = refs[6 : 6 + many]
        acc, kv = refs[6 + many : 8 + many]
        refs = refs[8 + many :]
    else:
        kv = refs[0]
        chunk_refs = refs[1 : 1 + many]
        acc = refs[2 + many]
        refs = refs[3 + many :]
    dq_refs = refs[:many]
    refs = refs[many:]
    if last:
        own_out, two_out, four_out, swap_out = refs[:4]
        refs = refs[4:]
    qa, ga, dqt = refs

    rows = chunk_refs[0].shape[0]
    width = GROUP * D
    scale = float(D) ** (-0.5)
    log2e = 1.4426950408889634

    if first:
        odd = ctx % 2 == 1
        kv[4 * block :, :] = own_ref[...]
        kv[2 * block : 3 * block, :] = two_ref[...]
        kv[:block, :] = four_ref[...]

        @pl.when(odd)
        def _():
            kv[3 * block : 4 * block, :] = p_own_ref[...]
            kv[block : 2 * block, :] = p_two_ref[...]

        @pl.when(jnp.logical_not(odd))
        def _():
            kv[3 * block : 4 * block, :] = p_two_ref[...]
            kv[block : 2 * block, :] = p_four_ref[...]

        acc[...] = jnp.zeros_like(acc)

    base = (ctx - LAGS) * block
    lane = lax.broadcasted_iota(jnp.int32, (rows, D), 1)
    part = lane // GROUP
    minus = jnp.where(
        lax.broadcasted_iota(jnp.int32, (TILE, D), 1) < 3 * GROUP, -1.0, 0.0
    ).astype(BF)
    key_iota = lax.broadcasted_iota(jnp.int32, (TILE, D), 0)
    token = lax.broadcasted_iota(jnp.int32, (1, D), 1) % rows

    for n, s in enumerate(shifts):
        src = me ^ s
        chunk = chunk_refs[n]
        first_pos = ctx * block + src * rows
        pos = first_pos + token
        low_first = jnp.int32(0)
        low = jnp.zeros_like(pos)
        begin = jnp.int32(0)
        for d in range(lens_ref.shape[0]):
            low_first = jnp.where(begin <= first_pos, begin, low_first)
            low = jnp.where(begin <= pos, begin, low)
            begin = begin + lens_ref[d]
        low = low - base
        high = pos - base
        lse = lse_ref[lanes(src * rows, rows), :] * (1.0 / scale)
        wide = jnp.zeros((rows, D), F32)
        for h in range(GROUP):
            wide = jnp.where(lane % GROUP == h, lse[:, h : h + 1], wide)
        hi, mid, lo3 = three_way(wide)
        zero = jnp.zeros_like(hi)
        lse3 = jnp.where(part == 0, hi, jnp.where(part == 1, mid, jnp.where(part == 2, lo3, zero)))
        del3 = chunk[:, 2 * width :]
        for h in range(GROUP):
            mine = lane % GROUP == h
            at = h * rows
            qa[at : at + rows, :D] = chunk[:, h * D : (h + 1) * D]
            qa[at : at + rows, D:] = jnp.where(mine, lse3, zero)
            ga[at : at + rows, :D] = chunk[:, width + h * D : width + (h + 1) * D]
            ga[at : at + rows, D:] = jnp.where(mine, del3, zero)
        dqt[...] = jnp.zeros_like(dqt)

        def tile_step(t, carry):
            at = pl.multiple_of(t * TILE, TILE)
            k_tile = kv[pl.ds(at, TILE), :D]
            v_tile = kv[pl.ds(at, TILE), D:]
            ka = jnp.concatenate([k_tile, minus], axis=1)
            va = jnp.concatenate([v_tile, minus], axis=1)
            key = key_iota + at
            ok = (key >= low) & (key <= high)
            okw = jnp.concatenate([ok] * (GROUP * rows // D), axis=1)
            st = lax.dot_general(ka, qa[...], NT, preferred_element_type=F32)
            w = jnp.where(okw, jnp.exp2(st * (scale * log2e)), 0.0)
            dp = lax.dot_general(va, ga[...], NT, preferred_element_type=F32)
            ds = (w * dp * scale).astype(BF)
            wb = w.astype(BF)
            acc[pl.ds(at, TILE), D:] += lax.dot_general(
                wb, ga[:, :D], NN, preferred_element_type=F32
            )
            acc[pl.ds(at, TILE), :D] += lax.dot_general(
                ds, qa[:, :D], NN, preferred_element_type=F32
            )
            dqt[...] += lax.dot_general(k_tile, ds, TN, preferred_element_type=F32)
            return carry

        t_lo = jnp.maximum(low_first - base, 0) // TILE
        t_hi = (first_pos + rows - 1 - base) // TILE
        lax.fori_loop(t_lo, t_hi + 1, tile_step, 0)
        dq = jnp.transpose(dqt[...])
        for h in range(GROUP):
            dq_refs[n][:, h * D : (h + 1) * D] = dq[h * rows : (h + 1) * rows, :].astype(BF)

    if last:
        own_out[...] = acc[4 * block :, :]
        two_out[...] = acc[2 * block : 3 * block, :]
        four_out[...] = acc[:block, :]
        swap_out[:block, :] = acc[block : 2 * block, :].astype(BF)
        swap_out[block:, :] = acc[3 * block : 4 * block, :].astype(BF)


def core_sum_body(own_ref, two_ref, four_ref, got_ref, own_out, two_out, four_out):
    block = own_ref.shape[0]
    odd = lax.axis_index("ctx") % 2 == 1
    far, near = got_ref[:block, :].astype(F32), got_ref[block:, :].astype(F32)
    zero = jnp.zeros_like(far)
    own_out[...] = own_ref[...] + jnp.where(odd, zero, near)
    two_out[...] = (two_ref[...] + jnp.where(odd, near, far)).astype(BF)
    four_out[...] = (four_ref[...] + jnp.where(odd, far, zero)).astype(BF)


def sum_body(heads, own_ref, two_ref, four_ref, *outs):
    me = lax.axis_index("head")
    rows = outs[0].shape[0]
    for s in range(heads):
        at = lanes((me ^ s) * rows, rows)
        total = own_ref[at, :] + two_ref[at, :].astype(F32) + four_ref[at, :].astype(F32)
        outs[s][...] = total.astype(BF)


def copy_all(pairs, sem):
    copies = [pltpu.make_async_copy(src, dst, sem.at[n]) for n, (src, dst) in enumerate(pairs)]
    for copy in copies:
        copy.start()
    for copy in copies:
        copy.wait()


def finish_q_body(heads, *refs):
    me = lax.axis_index("head")
    out, sem = refs[-2:]
    width = GROUP * D
    copy_all([(refs[s], out.at[:, lanes((me ^ s) * width, width)]) for s in range(heads)], sem)


def finish_kv_body(heads, *refs):
    me = lax.axis_index("head")
    dk, dv, sem = refs[-3:]
    pairs = []
    for s in range(heads):
        at = lanes((me ^ s) * D, D)
        pairs += [(refs[s].at[:, :D], dk.at[:, at]), (refs[s].at[:, D:], dv.at[:, at])]
    copy_all(pairs, sem)


def swap(x, s):
    n = lax.axis_size("head")
    return lax.ppermute(x, "head", [(i, i ^ s) for i in range(n)])


def along(x, distance):
    n = lax.axis_size("ctx")
    return lax.ppermute(x, "ctx", [(i, (i + distance) % n) for i in range(n)])


def other_core(x):
    n = lax.axis_size("ctx")
    return lax.ppermute(x, "ctx", [(i, i ^ 1) for i in range(n)])


def shape(*dims, dtype=BF):
    return jax.ShapeDtypeStruct(dims, dtype)


def call(
    body,
    outs,
    args,
    flops=0,
    scratch=(),
    smem=0,
    limit=4 << 20,
    hbm_in=False,
    hbm_out=False,
    aliases=None,
):
    nbytes = sum(a.size * a.dtype.itemsize for a in list(args) + list(outs))
    hbm = pl.BlockSpec(memory_space=pltpu.MemorySpace.HBM)
    ins = [hbm] * len(args) if hbm_in else vmem_specs(len(args) - smem)
    return pl.pallas_call(
        body,
        out_shape=list(outs),
        in_specs=[pl.BlockSpec(memory_space=pltpu.SMEM)] * smem + ins,
        out_specs=[hbm] * len(outs) if hbm_out else vmem_specs(len(outs)),
        scratch_shapes=list(scratch),
        cost_estimate=cost(flops, nbytes),
        input_output_aliases=aliases or {},
        compiler_params=pltpu.CompilerParams(vmem_limit_bytes=limit),
    )(*args)


def steps(queries, key_rows, value_rows, output_rows, output_grad, lse_rows, doc_lengths):
    rows = queries.shape[1]
    heads = lax.axis_size("head")
    block = rows * heads
    width = GROUP * D
    lse = lse_rows[0]

    qdo_out = call(
        functools.partial(pack_body, heads),
        [shape(rows, 2 * width + D)] * heads,
        [queries, output_grad, output_rows],
        limit=PACK_LIMIT,
        scratch=[pltpu.VMEM((heads, rows, width), BF), pltpu.SemaphoreType.DMA((3 * heads,))],
        hbm_in=True,
    )
    kv_out = call(
        functools.partial(pack_kv_body, heads), [shape(rows, 2 * D)] * heads, [key_rows, value_rows]
    )
    kv_in = [kv_out[0]] + [swap(kv_out[s], s) for s in range(1, heads)]
    chunks = [qdo_out[0]] + [swap(qdo_out[s], s) for s in range(1, heads)]
    (own,) = call(functools.partial(assemble_body, heads), [shape(block, 2 * D)], kv_in)
    p_own = other_core(own)
    two = along(own, 2)
    four = along(own, 4)
    p_two = other_core(two)
    p_four = other_core(four)
    kv_blocks = [own, two, four, p_own, p_two, p_four]

    total = (LAGS + 1) * block
    scratch = [
        pltpu.VMEM((GROUP * rows, 2 * D), BF),
        pltpu.VMEM((GROUP * rows, 2 * D), BF),
        pltpu.VMEM((D, GROUP * rows), F32),
    ]
    plan = [[0, 1], [2], [3]]
    dq = {}
    window = kv_blocks
    for n, shifts in enumerate(plan):
        first, last = n == 0, n == len(plan) - 1
        outs = [shape(total, 2 * D, dtype=F32)]
        if first:
            outs += [shape(total, 2 * D)]
        outs += [shape(rows, width)] * len(shifts)
        if last:
            outs += [shape(block, 2 * D, dtype=F32)] * 3 + [shape(2 * block, 2 * D)]
        args = [doc_lengths, lse] + window + [chunks[s] for s in shifts]
        aliases = None
        if not first:
            aliases = {len(args): 0}
            args.append(acc)
        res = call(
            functools.partial(compute_body, shifts, first, last, block),
            outs,
            args,
            flops=len(shifts) * 10 * total * rows * GROUP * D // 2,
            scratch=scratch,
            smem=1,
            limit=16 << 20,
            aliases=aliases,
        )
        acc = res[0]
        if first:
            window = [res[1]]
        for i, s in enumerate(shifts):
            dq[s] = res[(2 if first else 1) + i]
        rest = res[1 + len(shifts) :]
    d_own, d_two, d_four, d_swap = rest
    got = other_core(d_swap)
    d_own, d_two, d_four = call(
        core_sum_body,
        [shape(block, 2 * D, dtype=F32)] + [shape(block, 2 * D)] * 2,
        [d_own, d_two, d_four, got],
    )
    back_two, back_four = along(d_two, -2), along(d_four, -4)
    dq_in = [dq[0]] + [swap(dq[s], s) for s in range(1, heads)]
    sums = call(
        functools.partial(sum_body, heads),
        [shape(rows, 2 * D)] * heads,
        [d_own, back_two, back_four],
    )
    (query_grad,) = call(
        functools.partial(finish_q_body, heads),
        [shape(rows, heads * width)],
        dq_in,
        scratch=[pltpu.SemaphoreType.DMA((heads,))],
        hbm_out=True,
    )
    kv_grad = [sums[0]] + [swap(sums[s], s) for s in range(1, heads)]
    dk, dv = call(
        functools.partial(finish_kv_body, heads),
        [shape(rows, heads * D)] * 2,
        kv_grad,
        scratch=[pltpu.SemaphoreType.DMA((2 * heads,))],
        hbm_out=True,
    )
    return query_grad[None], dk[None], dv[None]


def solution(mesh):
    in_specs = (
        P("ctx", "head", None),
        P("ctx", "head", None),
        P("ctx", "head", None),
        P("ctx", "head", None),
        P("ctx", "head", None),
        P("ctx", None, "head"),
        P(),
    )
    out_specs = (P("ctx", "head", None), P("ctx", "head", None), P("ctx", "head", None))
    return jax.shard_map(steps, mesh=mesh, in_specs=in_specs, out_specs=out_specs, check_vma=False)
```

```python
import functools

import jax
import jax.numpy as jnp
from jax import lax
from jax.experimental import pallas as pl
from jax.experimental.pallas import tpu as pltpu
from jax.sharding import PartitionSpec as P


QUERY_HEAD_COUNT = 32
KEY_VALUE_HEADS = 4
GROUP = QUERY_HEAD_COUNT // KEY_VALUE_HEADS
D = 128
LAGS = 4
TILE = 256
PACK_LIMIT = 55000000
BF = jnp.bfloat16
F32 = jnp.float32
NT = (((1,), (1,)), ((), ()))
NN = (((1,), (0,)), ((), ()))
TN = (((0,), (0,)), ((), ()))


def lanes(start, size):
    return pl.ds(pl.multiple_of(start, size), size)


def vmem_specs(count):
    return [pl.BlockSpec(memory_space=pltpu.VMEM)] * count


def cost(flops, nbytes):
    return pl.CostEstimate(flops=flops, bytes_accessed=nbytes, transcendentals=0)


def three_way(x):
    hi = x.astype(BF)
    rest = x - hi.astype(F32)
    mid = rest.astype(BF)
    low = (rest - mid.astype(F32)).astype(BF)
    return hi, mid, low


def pack_kv_body(heads, k_ref, v_ref, *outs):
    me = lax.axis_index("head")
    for s in range(heads):
        at = lanes((me ^ s) * D, D)
        outs[s][:, :D] = k_ref[0, :, at]
        outs[s][:, D:] = v_ref[0, :, at]


def pack_body(heads, q_ref, g_ref, o_ref, *refs):
    q_ref, g_ref, o_ref = (ref.at[0] for ref in (q_ref, g_ref, o_ref))
    outs, (o_buf, sem) = refs[:heads], refs[heads:]
    me = lax.axis_index("head")
    rows = q_ref.shape[0]
    pairs = GROUP // 2
    wide = 2 * D
    copies = {}
    count = 0
    shifts = list(range(1, heads)) + [0]
    for s, names in [(s, "og") for s in shifts] + [(s, "q") for s in shifts]:
        start = (me ^ s) * (pairs * wide)
        for name in names:
            for p in range(1 if name == "o" else pairs):
                cols = lanes(start + p * wide, wide)
                if name == "o":
                    cols = lanes(start, pairs * wide)
                    src, dst = o_ref.at[:, cols], o_buf.at[s]
                elif name == "g":
                    src, dst = g_ref.at[:, cols], outs[s].at[pl.ds((pairs + p) * rows, rows)]
                else:
                    src, dst = q_ref.at[:, cols], outs[s].at[pl.ds(p * rows, rows)]
                copies[s, name, p] = pltpu.make_async_copy(src, dst, sem.at[count])
                copies[s, name, p].start()
                count += 1
    lane = lax.broadcasted_iota(jnp.int32, (2 * rows, D), 1)
    side = lax.broadcasted_iota(jnp.int32, (GROUP, D), 1) < rows
    for s in shifts:
        copies[s, "o", 0].wait()
        for p in range(pairs):
            copies[s, "g", p].wait()
        delta = jnp.zeros((rows, D), F32)
        for p in range(pairs):
            grad = outs[s][(pairs + p) * rows : (pairs + p + 1) * rows, :]
            prod = grad.astype(F32) * o_buf[s, :, p * wide : (p + 1) * wide].astype(F32)
            for h in range(2):
                one = jnp.sum(prod[:, h * D : (h + 1) * D], axis=1, keepdims=True)
                delta = jnp.where(lane[:rows] == 2 * p + h, one, delta)
        turned = jnp.transpose(jnp.concatenate([delta, delta], axis=0))[:GROUP, :]
        hi, mid, low = three_way(turned)
        outs[s][GROUP * rows :, :D] = jnp.where(side, hi, mid)
        outs[s][GROUP * rows :, D:] = jnp.where(side, low, jnp.zeros_like(low))
    for s in range(heads):
        for p in range(pairs):
            copies[s, "q", p].wait()


def assemble_body(heads, *refs):
    me = lax.axis_index("head")
    out = refs[-1]
    rows = refs[0].shape[0]
    for s in range(heads):
        out[lanes((me ^ s) * rows, rows), :] = refs[s][...]


def compute_body(shifts, first, last, block, lens_ref, lse_ref, *refs):
    me = lax.axis_index("head")
    ctx = lax.axis_index("ctx")
    refs = list(refs)
    many = len(shifts)
    if first:
        own_ref, two_ref, four_ref, p_own_ref, p_two_ref, p_four_ref = refs[:6]
        chunk_refs = refs[6 : 6 + many]
        acc, kv = refs[6 + many : 8 + many]
        refs = refs[8 + many :]
    else:
        kv = refs[0]
        chunk_refs = refs[1 : 1 + many]
        acc = refs[2 + many]
        refs = refs[3 + many :]
    dq_refs = refs[:many]
    refs = refs[many:]
    if last:
        swap_out = refs.pop(0)
    qa, ga, dqt = refs

    rows = chunk_refs[0].shape[0] // GROUP - 1
    scale = float(D) ** (-0.5)
    log2e = 1.4426950408889634

    if first:
        odd = ctx % 2 == 1
        kv[4 * block :, :] = own_ref[...]
        kv[2 * block : 3 * block, :] = two_ref[...]
        kv[:block, :] = four_ref[...]

        @pl.when(odd)
        def _():
            kv[3 * block : 4 * block, :] = p_own_ref[...]
            kv[block : 2 * block, :] = p_two_ref[...]

        @pl.when(jnp.logical_not(odd))
        def _():
            kv[3 * block : 4 * block, :] = p_two_ref[...]
            kv[block : 2 * block, :] = p_four_ref[...]

        acc[...] = jnp.zeros_like(acc)

    base = (ctx - LAGS) * block
    lane = lax.broadcasted_iota(jnp.int32, (rows, D), 1)
    part = lane // GROUP
    minus = jnp.where(
        lax.broadcasted_iota(jnp.int32, (TILE, D), 1) < 3 * GROUP, -1.0, 0.0
    ).astype(BF)
    key_iota = lax.broadcasted_iota(jnp.int32, (TILE, D), 0)
    token = lax.broadcasted_iota(jnp.int32, (1, D), 1) % rows

    for n, s in enumerate(shifts):
        src = me ^ s
        chunk = chunk_refs[n]
        first_pos = ctx * block + src * rows
        pos = first_pos + token
        low_first = jnp.int32(0)
        low = jnp.zeros_like(pos)
        begin = jnp.int32(0)
        for d in range(lens_ref.shape[0]):
            low_first = jnp.where(begin <= first_pos, begin, low_first)
            low = jnp.where(begin <= pos, begin, low)
            begin = begin + lens_ref[d]
        low = low - base
        high = pos - base
        lse = lse_ref[lanes(src * rows, rows), :] * (1.0 / scale)
        wide = jnp.zeros((rows, D), F32)
        for h in range(GROUP):
            wide = jnp.where(lane % GROUP == h, lse[:, h : h + 1], wide)
        hi, mid, lo3 = three_way(wide)
        zero = jnp.zeros_like(hi)
        lse3 = jnp.where(part == 0, hi, jnp.where(part == 1, mid, jnp.where(part == 2, lo3, zero)))
        end = GROUP * rows
        upper = chunk[end : end + GROUP, :D].astype(F32)
        lower = chunk[end : end + GROUP, D:].astype(F32)
        stack = [upper, lower, upper, jnp.zeros((D - 3 * GROUP, D), F32)]
        turned = jnp.transpose(jnp.concatenate(stack, axis=0)).astype(BF)
        del3 = jnp.where(
            part < 2, turned[:rows, :], jnp.where(part == 2, turned[rows:, :], zero)
        )
        for h in range(GROUP):
            mine = lane % GROUP == h
            at, half = h * rows, (h % 2) * D
            off = h // 2 * rows
            qa[at : at + rows, :D] = chunk[off : off + rows, half : half + D]
            qa[at : at + rows, D:] = jnp.where(mine, lse3, zero)
            off += GROUP // 2 * rows
            ga[at : at + rows, :D] = chunk[off : off + rows, half : half + D]
            ga[at : at + rows, D:] = jnp.where(mine, del3, zero)
        dqt[...] = jnp.zeros_like(dqt)

        def tile_terms(at):
            k_tile = kv[pl.ds(at, TILE), :D]
            v_tile = kv[pl.ds(at, TILE), D:]
            ka = jnp.concatenate([k_tile, minus], axis=1)
            va = jnp.concatenate([v_tile, minus], axis=1)
            key = key_iota + at
            ok = (key >= low) & (key <= high)
            okw = jnp.concatenate([ok] * (GROUP * rows // D), axis=1)
            st = lax.dot_general(ka, qa[...], NT, preferred_element_type=F32)
            w = jnp.where(okw, jnp.exp2(st * (scale * log2e)), 0.0)
            dp = lax.dot_general(va, ga[...], NT, preferred_element_type=F32)
            return k_tile, w.astype(BF), (w * dp * scale).astype(BF)

        def tile_adds(at, terms):
            k_tile, wb, ds = terms
            acc[pl.ds(at, TILE), D:] += lax.dot_general(
                wb, ga[:, :D], NN, preferred_element_type=F32
            )
            acc[pl.ds(at, TILE), :D] += lax.dot_general(
                ds, qa[:, :D], NN, preferred_element_type=F32
            )
            return lax.dot_general(k_tile, ds, TN, preferred_element_type=F32)

        def one_tile(t):
            at = pl.multiple_of(t * TILE, TILE)
            dqt[...] += tile_adds(at, tile_terms(at))

        t_lo = jnp.maximum(low_first - base, 0) // TILE
        count = (first_pos + rows - 1 - base) // TILE + 1 - t_lo

        def two_tiles(i, carry):
            at = pl.multiple_of((t_lo + 2 * i) * TILE, TILE)
            then = pl.multiple_of((t_lo + 2 * i + 1) * TILE, TILE)
            here, there = tile_terms(at), tile_terms(then)
            dqt[...] += tile_adds(at, here) + tile_adds(then, there)
            return carry

        lax.fori_loop(0, count // 2, two_tiles, 0)

        @pl.when(count % 2 == 1)
        def _():
            one_tile(t_lo + count - 1)

        dq = jnp.transpose(dqt[...])
        for h in range(GROUP):
            dq_refs[n][:, h * D : (h + 1) * D] = dq[h * rows : (h + 1) * rows, :].astype(BF)

    if last:
        swap_out[:block, :] = acc[block : 2 * block, :].astype(BF)
        swap_out[block:, :] = acc[3 * block : 4 * block, :].astype(BF)


def core_sum_body(acc, got_ref, own_out, two_out, four_out):
    block = own_out.shape[0]
    odd = lax.axis_index("ctx") % 2 == 1
    far, near = got_ref[:block, :].astype(F32), got_ref[block:, :].astype(F32)
    zero = jnp.zeros_like(far)
    own_out[...] = acc[4 * block :, :] + jnp.where(odd, zero, near)
    two_out[...] = (acc[2 * block : 3 * block, :] + jnp.where(odd, near, far)).astype(BF)
    four_out[...] = (acc[:block, :] + jnp.where(odd, far, zero)).astype(BF)


def sum_body(heads, own_ref, two_ref, four_ref, *outs):
    me = lax.axis_index("head")
    rows = outs[0].shape[0]
    for s in range(heads):
        at = lanes((me ^ s) * rows, rows)
        total = own_ref[at, :] + two_ref[at, :].astype(F32) + four_ref[at, :].astype(F32)
        outs[s][...] = total.astype(BF)


def copy_all(pairs, sem):
    copies = [pltpu.make_async_copy(src, dst, sem.at[n]) for n, (src, dst) in enumerate(pairs)]
    for copy in copies:
        copy.start()
    for copy in copies:
        copy.wait()


def finish_q_body(heads, *refs):
    me = lax.axis_index("head")
    out, sem = refs[-2:]
    width = GROUP * D
    copy_all([(refs[s], out.at[:, lanes((me ^ s) * width, width)]) for s in range(heads)], sem)


def finish_kv_body(heads, *refs):
    me = lax.axis_index("head")
    dk, dv, sem = refs[-3:]
    pairs = []
    for s in range(heads):
        at = lanes((me ^ s) * D, D)
        pairs += [(refs[s].at[:, :D], dk.at[:, at]), (refs[s].at[:, D:], dv.at[:, at])]
    copy_all(pairs, sem)


def swap(x, s):
    n = lax.axis_size("head")
    return lax.ppermute(x, "head", [(i, i ^ s) for i in range(n)])


def along(x, distance):
    n = lax.axis_size("ctx")
    return lax.ppermute(x, "ctx", [(i, (i + distance) % n) for i in range(n)])


def other_core(x):
    n = lax.axis_size("ctx")
    return lax.ppermute(x, "ctx", [(i, i ^ 1) for i in range(n)])


def shape(*dims, dtype=BF):
    return jax.ShapeDtypeStruct(dims, dtype)


def call(
    body,
    outs,
    args,
    flops=0,
    scratch=(),
    smem=0,
    limit=4 << 20,
    hbm_in=False,
    hbm_out=False,
    aliases=None,
):
    nbytes = sum(a.size * a.dtype.itemsize for a in list(args) + list(outs))
    hbm = pl.BlockSpec(memory_space=pltpu.MemorySpace.HBM)
    ins = [hbm] * len(args) if hbm_in else vmem_specs(len(args) - smem)
    return pl.pallas_call(
        body,
        out_shape=list(outs),
        in_specs=[pl.BlockSpec(memory_space=pltpu.SMEM)] * smem + ins,
        out_specs=[hbm] * len(outs) if hbm_out else vmem_specs(len(outs)),
        scratch_shapes=list(scratch),
        cost_estimate=cost(flops, nbytes),
        input_output_aliases=aliases or {},
        compiler_params=pltpu.CompilerParams(vmem_limit_bytes=limit),
    )(*args)


def steps(queries, key_rows, value_rows, output_rows, output_grad, lse_rows, doc_lengths):
    rows = queries.shape[1]
    heads = lax.axis_size("head")
    block = rows * heads
    width = GROUP * D
    lse = lse_rows[0]

    qdo_out = call(
        functools.partial(pack_body, heads),
        [shape(GROUP * rows + GROUP, 2 * D)] * heads,
        [queries, output_grad, output_rows],
        limit=PACK_LIMIT,
        scratch=[
            pltpu.VMEM((heads, rows, width), BF),
            pltpu.SemaphoreType.DMA((heads * (GROUP + 1),)),
        ],
        hbm_in=True,
    )
    kv_out = call(
        functools.partial(pack_kv_body, heads), [shape(rows, 2 * D)] * heads, [key_rows, value_rows]
    )
    kv_in = [kv_out[0]] + [swap(kv_out[s], s) for s in range(1, heads)]
    chunks = [qdo_out[0]] + [swap(qdo_out[s], s) for s in range(1, heads)]
    (own,) = call(functools.partial(assemble_body, heads), [shape(block, 2 * D)], kv_in)
    p_own = other_core(own)
    two = along(own, 2)
    four = along(own, 4)
    p_two = other_core(two)
    p_four = other_core(four)
    kv_blocks = [own, two, four, p_own, p_two, p_four]

    total = (LAGS + 1) * block
    scratch = [
        pltpu.VMEM((GROUP * rows, 2 * D), BF),
        pltpu.VMEM((GROUP * rows, 2 * D), BF),
        pltpu.VMEM((D, GROUP * rows), F32),
    ]
    plan = [[0, 1], [2], [3]]
    dq = {}
    window = kv_blocks
    for n, shifts in enumerate(plan):
        first, last = n == 0, n == len(plan) - 1
        outs = [shape(total, 2 * D, dtype=F32)]
        if first:
            outs += [shape(total, 2 * D)]
        outs += [shape(rows, width)] * len(shifts)
        if last:
            outs += [shape(2 * block, 2 * D)]
        args = [doc_lengths, lse] + window + [chunks[s] for s in shifts]
        aliases = None
        if not first:
            aliases = {len(args): 0}
            args.append(acc)
        res = call(
            functools.partial(compute_body, shifts, first, last, block),
            outs,
            args,
            flops=len(shifts) * 10 * total * rows * GROUP * D // 2,
            scratch=scratch,
            smem=1,
            limit=16 << 20,
            aliases=aliases,
        )
        acc = res[0]
        if first:
            window = [res[1]]
        for i, s in enumerate(shifts):
            dq[s] = res[(2 if first else 1) + i]
        rest = res[1 + len(shifts) :]
    (d_swap,) = rest
    got = other_core(d_swap)
    d_own, d_two, d_four = call(
        core_sum_body, [shape(block, 2 * D, dtype=F32)] + [shape(block, 2 * D)] * 2, [acc, got]
    )
    back_two, back_four = along(d_two, -2), along(d_four, -4)
    dq_in = [dq[0]] + [swap(dq[s], s) for s in range(1, heads)]
    sums = call(
        functools.partial(sum_body, heads),
        [shape(rows, 2 * D)] * heads,
        [d_own, back_two, back_four],
    )
    (query_grad,) = call(
        functools.partial(finish_q_body, heads),
        [shape(rows, heads * width)],
        dq_in,
        scratch=[pltpu.SemaphoreType.DMA((heads,))],
        hbm_out=True,
    )
    kv_grad = [sums[0]] + [swap(sums[s], s) for s in range(1, heads)]
    dk, dv = call(
        functools.partial(finish_kv_body, heads),
        [shape(rows, heads * D)] * 2,
        kv_grad,
        scratch=[pltpu.SemaphoreType.DMA((2 * heads,))],
        hbm_out=True,
    )
    return query_grad[None], dk[None], dv[None]


def solution(mesh):
    in_specs = (
        P("ctx", "head", None),
        P("ctx", "head", None),
        P("ctx", "head", None),
        P("ctx", "head", None),
        P("ctx", "head", None),
        P("ctx", None, "head"),
        P(),
    )
    out_specs = (P("ctx", "head", None), P("ctx", "head", None), P("ctx", "head", None))
    return jax.shard_map(steps, mesh=mesh, in_specs=in_specs, out_specs=out_specs, check_vma=False)
```

```python
import functools

import jax
import jax.numpy as jnp
from jax import lax
from jax.experimental import pallas as pl
from jax.experimental.pallas import tpu as pltpu
from jax.sharding import PartitionSpec as P


QUERY_HEAD_COUNT = 32
KEY_VALUE_HEADS = 4
GROUP = QUERY_HEAD_COUNT // KEY_VALUE_HEADS
D = 128
LAGS = 4
TILE = 256
PACK_LIMIT = 55000000
BF = jnp.bfloat16
F32 = jnp.float32
NT = (((1,), (1,)), ((), ()))
NN = (((1,), (0,)), ((), ()))
TN = (((0,), (0,)), ((), ()))


def lanes(start, size):
    return pl.ds(pl.multiple_of(start, size), size)


def vmem_specs(count):
    return [pl.BlockSpec(memory_space=pltpu.VMEM)] * count


def cost(flops, nbytes):
    return pl.CostEstimate(flops=flops, bytes_accessed=nbytes, transcendentals=0)


def three_way(x):
    hi = x.astype(BF)
    rest = x - hi.astype(F32)
    mid = rest.astype(BF)
    low = (rest - mid.astype(F32)).astype(BF)
    return hi, mid, low


def pack_kv_body(heads, k_ref, v_ref, *outs):
    me = lax.axis_index("head")
    for s in range(heads):
        at = lanes((me ^ s) * D, D)
        outs[s][:, :D] = k_ref[0, :, at]
        outs[s][:, D:] = v_ref[0, :, at]


def pack_body(heads, q_ref, g_ref, o_ref, *refs):
    q_ref, g_ref, o_ref = (ref.at[0] for ref in (q_ref, g_ref, o_ref))
    outs, (o_buf, sem) = refs[:heads], refs[heads:]
    me = lax.axis_index("head")
    rows = q_ref.shape[0]
    pairs = GROUP // 2
    wide = 2 * D
    copies = {}
    count = 0
    shifts = list(range(1, heads)) + [0]
    for s, names in [(s, "og") for s in shifts] + [(s, "q") for s in shifts]:
        start = (me ^ s) * (pairs * wide)
        for name in names:
            for p in range(1 if name == "o" else pairs):
                cols = lanes(start + p * wide, wide)
                if name == "o":
                    cols = lanes(start, pairs * wide)
                    src, dst = o_ref.at[:, cols], o_buf.at[s]
                elif name == "g":
                    src, dst = g_ref.at[:, cols], outs[s].at[pl.ds((pairs + p) * rows, rows)]
                else:
                    src, dst = q_ref.at[:, cols], outs[s].at[pl.ds(p * rows, rows)]
                copies[s, name, p] = pltpu.make_async_copy(src, dst, sem.at[count])
                copies[s, name, p].start()
                count += 1
    lane = lax.broadcasted_iota(jnp.int32, (2 * rows, D), 1)
    side = lax.broadcasted_iota(jnp.int32, (GROUP, D), 1) < rows
    deltas = []
    for s in shifts:
        copies[s, "o", 0].wait()
        for p in range(pairs):
            copies[s, "g", p].wait()
        delta = jnp.zeros((rows, D), F32)
        for p in range(pairs):
            grad = outs[s][(pairs + p) * rows : (pairs + p + 1) * rows, :]
            prod = grad.astype(F32) * o_buf[s, :, p * wide : (p + 1) * wide].astype(F32)
            for h in range(2):
                one = jnp.sum(prod[:, h * D : (h + 1) * D], axis=1, keepdims=True)
                delta = jnp.where(lane[:rows] == 2 * p + h, one, delta)
        deltas.append(delta)
    turns = [jnp.transpose(jnp.concatenate([delta, delta], axis=0)) for delta in deltas]
    for s, turned in zip(shifts, turns):
        hi, mid, low = three_way(turned[:GROUP, :])
        outs[s][GROUP * rows :, :D] = jnp.where(side, hi, mid)
        outs[s][GROUP * rows :, D:] = jnp.where(side, low, jnp.zeros_like(low))
    for s in range(heads):
        for p in range(pairs):
            copies[s, "q", p].wait()


def assemble_body(heads, *refs):
    me = lax.axis_index("head")
    out = refs[-1]
    rows = refs[0].shape[0]
    for s in range(heads):
        out[lanes((me ^ s) * rows, rows), :] = refs[s][...]


def compute_body(shifts, first, last, block, lens_ref, lse_ref, *refs):
    me = lax.axis_index("head")
    ctx = lax.axis_index("ctx")
    refs = list(refs)
    many = len(shifts)
    if first:
        own_ref, two_ref, four_ref, p_own_ref, p_two_ref, p_four_ref = refs[:6]
        chunk_refs = refs[6 : 6 + many]
        acc, kv = refs[6 + many : 8 + many]
        refs = refs[8 + many :]
    else:
        kv = refs[0]
        chunk_refs = refs[1 : 1 + many]
        acc = refs[2 + many]
        refs = refs[3 + many :]
    dq_refs = refs[:many]
    refs = refs[many:]
    if last:
        swap_out = refs.pop(0)
    qa, ga, dqt = refs

    rows = chunk_refs[0].shape[0] // GROUP - 1
    scale = float(D) ** (-0.5)
    log2e = 1.4426950408889634

    if first:
        odd = ctx % 2 == 1
        kv[4 * block :, :] = own_ref[...]
        kv[2 * block : 3 * block, :] = two_ref[...]
        kv[:block, :] = four_ref[...]

        @pl.when(odd)
        def _():
            kv[3 * block : 4 * block, :] = p_own_ref[...]
            kv[block : 2 * block, :] = p_two_ref[...]

        @pl.when(jnp.logical_not(odd))
        def _():
            kv[3 * block : 4 * block, :] = p_two_ref[...]
            kv[block : 2 * block, :] = p_four_ref[...]

        acc[...] = jnp.zeros_like(acc)

    base = (ctx - LAGS) * block
    lane = lax.broadcasted_iota(jnp.int32, (rows, D), 1)
    part = lane // GROUP
    minus = jnp.where(
        lax.broadcasted_iota(jnp.int32, (TILE, D), 1) < 3 * GROUP, -1.0, 0.0
    ).astype(BF)
    key_iota = lax.broadcasted_iota(jnp.int32, (TILE, D), 0)
    token = lax.broadcasted_iota(jnp.int32, (1, D), 1) % rows

    for n, s in enumerate(shifts):
        src = me ^ s
        chunk = chunk_refs[n]
        first_pos = ctx * block + src * rows
        pos = first_pos + token
        low_first = jnp.int32(0)
        low = jnp.zeros_like(pos)
        begin = jnp.int32(0)
        for d in range(lens_ref.shape[0]):
            low_first = jnp.where(begin <= first_pos, begin, low_first)
            low = jnp.where(begin <= pos, begin, low)
            begin = begin + lens_ref[d]
        low = low - base
        high = pos - base
        lse = lse_ref[lanes(src * rows, rows), :] * (1.0 / scale)
        wide = jnp.zeros((rows, D), F32)
        for h in range(GROUP):
            wide = jnp.where(lane % GROUP == h, lse[:, h : h + 1], wide)
        hi, mid, lo3 = three_way(wide)
        zero = jnp.zeros_like(hi)
        lse3 = jnp.where(part == 0, hi, jnp.where(part == 1, mid, jnp.where(part == 2, lo3, zero)))
        end = GROUP * rows
        upper = chunk[end : end + GROUP, :D].astype(F32)
        lower = chunk[end : end + GROUP, D:].astype(F32)
        stack = [upper, lower, upper, jnp.zeros((D - 3 * GROUP, D), F32)]
        turned = jnp.transpose(jnp.concatenate(stack, axis=0)).astype(BF)
        del3 = jnp.where(
            part < 2, turned[:rows, :], jnp.where(part == 2, turned[rows:, :], zero)
        )
        for h in range(GROUP):
            mine = lane % GROUP == h
            at, half = h * rows, (h % 2) * D
            off = h // 2 * rows
            qa[at : at + rows, :D] = chunk[off : off + rows, half : half + D]
            qa[at : at + rows, D:] = jnp.where(mine, lse3, zero)
            off += GROUP // 2 * rows
            ga[at : at + rows, :D] = chunk[off : off + rows, half : half + D]
            ga[at : at + rows, D:] = jnp.where(mine, del3, zero)
        dqt[...] = jnp.zeros_like(dqt)

        def tile_terms(at):
            k_tile = kv[pl.ds(at, TILE), :D]
            v_tile = kv[pl.ds(at, TILE), D:]
            ka = jnp.concatenate([k_tile, minus], axis=1)
            va = jnp.concatenate([v_tile, minus], axis=1)
            key = key_iota + at
            ok = (key >= low) & (key <= high)
            okw = jnp.concatenate([ok] * (GROUP * rows // D), axis=1)
            st = lax.dot_general(ka, qa[...], NT, preferred_element_type=F32)
            w = jnp.where(okw, jnp.exp2(st * (scale * log2e)), 0.0)
            dp = lax.dot_general(va, ga[...], NT, preferred_element_type=F32)
            return k_tile, w.astype(BF), (w * dp * scale).astype(BF)

        def tile_adds(at, terms):
            k_tile, wb, ds = terms
            acc[pl.ds(at, TILE), D:] += lax.dot_general(
                wb, ga[:, :D], NN, preferred_element_type=F32
            )
            acc[pl.ds(at, TILE), :D] += lax.dot_general(
                ds, qa[:, :D], NN, preferred_element_type=F32
            )
            return lax.dot_general(k_tile, ds, TN, preferred_element_type=F32)

        def one_tile(t):
            at = pl.multiple_of(t * TILE, TILE)
            dqt[...] += tile_adds(at, tile_terms(at))

        t_lo = jnp.maximum(low_first - base, 0) // TILE
        count = (first_pos + rows - 1 - base) // TILE + 1 - t_lo

        def two_tiles(i, carry):
            at = pl.multiple_of((t_lo + 2 * i) * TILE, TILE)
            then = pl.multiple_of((t_lo + 2 * i + 1) * TILE, TILE)
            here, there = tile_terms(at), tile_terms(then)
            dqt[...] += tile_adds(at, here) + tile_adds(then, there)
            return carry

        lax.fori_loop(0, count // 2, two_tiles, 0)

        @pl.when(count % 2 == 1)
        def _():
            one_tile(t_lo + count - 1)

        dq = jnp.transpose(dqt[...])
        for h in range(GROUP):
            dq_refs[n][:, h * D : (h + 1) * D] = dq[h * rows : (h + 1) * rows, :].astype(BF)

    if last:
        swap_out[:block, :] = acc[block : 2 * block, :].astype(BF)
        swap_out[block:, :] = acc[3 * block : 4 * block, :].astype(BF)


def core_sum_body(acc, got_ref, own_out, two_out, four_out):
    block = own_out.shape[0]
    odd = lax.axis_index("ctx") % 2 == 1
    far, near = got_ref[:block, :].astype(F32), got_ref[block:, :].astype(F32)
    zero = jnp.zeros_like(far)
    own_out[...] = acc[4 * block :, :] + jnp.where(odd, zero, near)
    two_out[...] = (acc[2 * block : 3 * block, :] + jnp.where(odd, near, far)).astype(BF)
    four_out[...] = (acc[:block, :] + jnp.where(odd, far, zero)).astype(BF)


def sum_body(heads, own_ref, two_ref, four_ref, *outs):
    me = lax.axis_index("head")
    rows = outs[0].shape[0]
    for s in range(heads):
        at = lanes((me ^ s) * rows, rows)
        total = own_ref[at, :] + two_ref[at, :].astype(F32) + four_ref[at, :].astype(F32)
        outs[s][...] = total.astype(BF)


def copy_all(pairs, sem):
    copies = [pltpu.make_async_copy(src, dst, sem.at[n]) for n, (src, dst) in enumerate(pairs)]
    for copy in copies:
        copy.start()
    for copy in copies:
        copy.wait()


def finish_q_body(heads, *refs):
    me = lax.axis_index("head")
    out, sem = refs[-2:]
    width = GROUP * D
    copy_all([(refs[s], out.at[:, lanes((me ^ s) * width, width)]) for s in range(heads)], sem)


def finish_kv_body(heads, *refs):
    me = lax.axis_index("head")
    dk, dv, sem = refs[-3:]
    pairs = []
    for s in range(heads):
        at = lanes((me ^ s) * D, D)
        pairs += [(refs[s].at[:, :D], dk.at[:, at]), (refs[s].at[:, D:], dv.at[:, at])]
    copy_all(pairs, sem)


def swap(x, s):
    n = lax.axis_size("head")
    return lax.ppermute(x, "head", [(i, i ^ s) for i in range(n)])


def along(x, distance):
    n = lax.axis_size("ctx")
    return lax.ppermute(x, "ctx", [(i, (i + distance) % n) for i in range(n)])


def other_core(x):
    n = lax.axis_size("ctx")
    return lax.ppermute(x, "ctx", [(i, i ^ 1) for i in range(n)])


def shape(*dims, dtype=BF):
    return jax.ShapeDtypeStruct(dims, dtype)


def call(
    body,
    outs,
    args,
    flops=0,
    scratch=(),
    smem=0,
    limit=4 << 20,
    hbm_in=False,
    hbm_out=False,
    aliases=None,
):
    nbytes = sum(a.size * a.dtype.itemsize for a in list(args) + list(outs))
    hbm = pl.BlockSpec(memory_space=pltpu.MemorySpace.HBM)
    ins = [hbm] * len(args) if hbm_in else vmem_specs(len(args) - smem)
    return pl.pallas_call(
        body,
        out_shape=list(outs),
        in_specs=[pl.BlockSpec(memory_space=pltpu.SMEM)] * smem + ins,
        out_specs=[hbm] * len(outs) if hbm_out else vmem_specs(len(outs)),
        scratch_shapes=list(scratch),
        cost_estimate=cost(flops, nbytes),
        input_output_aliases=aliases or {},
        compiler_params=pltpu.CompilerParams(vmem_limit_bytes=limit),
    )(*args)


def steps(queries, key_rows, value_rows, output_rows, output_grad, lse_rows, doc_lengths):
    rows = queries.shape[1]
    heads = lax.axis_size("head")
    block = rows * heads
    width = GROUP * D
    lse = lse_rows[0]

    qdo_out = call(
        functools.partial(pack_body, heads),
        [shape(GROUP * rows + GROUP, 2 * D)] * heads,
        [queries, output_grad, output_rows],
        limit=PACK_LIMIT,
        scratch=[
            pltpu.VMEM((heads, rows, width), BF),
            pltpu.SemaphoreType.DMA((heads * (GROUP + 1),)),
        ],
        hbm_in=True,
    )
    kv_out = call(
        functools.partial(pack_kv_body, heads), [shape(rows, 2 * D)] * heads, [key_rows, value_rows]
    )
    kv_in = [kv_out[0]] + [swap(kv_out[s], s) for s in range(1, heads)]
    chunks = [qdo_out[0]] + [swap(qdo_out[s], s) for s in range(1, heads)]
    (own,) = call(functools.partial(assemble_body, heads), [shape(block, 2 * D)], kv_in)
    p_own = other_core(own)
    two = along(own, 2)
    four = along(own, 4)
    p_two = other_core(two)
    p_four = other_core(four)
    kv_blocks = [own, two, four, p_own, p_two, p_four]

    total = (LAGS + 1) * block
    scratch = [
        pltpu.VMEM((GROUP * rows, 2 * D), BF),
        pltpu.VMEM((GROUP * rows, 2 * D), BF),
        pltpu.VMEM((D, GROUP * rows), F32),
    ]
    plan = [[0, 1], [2], [3]]
    dq = {}
    window = kv_blocks
    for n, shifts in enumerate(plan):
        first, last = n == 0, n == len(plan) - 1
        outs = [shape(total, 2 * D, dtype=F32)]
        if first:
            outs += [shape(total, 2 * D)]
        outs += [shape(rows, width)] * len(shifts)
        if last:
            outs += [shape(2 * block, 2 * D)]
        args = [doc_lengths, lse] + window + [chunks[s] for s in shifts]
        aliases = None
        if not first:
            aliases = {len(args): 0}
            args.append(acc)
        res = call(
            functools.partial(compute_body, shifts, first, last, block),
            outs,
            args,
            flops=len(shifts) * 10 * total * rows * GROUP * D // 2,
            scratch=scratch,
            smem=1,
            limit=16 << 20,
            aliases=aliases,
        )
        acc = res[0]
        if first:
            window = [res[1]]
        for i, s in enumerate(shifts):
            dq[s] = res[(2 if first else 1) + i]
        rest = res[1 + len(shifts) :]
    (d_swap,) = rest
    got = other_core(d_swap)
    d_own, d_two, d_four = call(
        core_sum_body, [shape(block, 2 * D, dtype=F32)] + [shape(block, 2 * D)] * 2, [acc, got]
    )
    back_two, back_four = along(d_two, -2), along(d_four, -4)
    dq_in = [dq[0]] + [swap(dq[s], s) for s in range(1, heads)]
    sums = call(
        functools.partial(sum_body, heads),
        [shape(rows, 2 * D)] * heads,
        [d_own, back_two, back_four],
    )
    (query_grad,) = call(
        functools.partial(finish_q_body, heads),
        [shape(rows, heads * width)],
        dq_in,
        scratch=[pltpu.SemaphoreType.DMA((heads,))],
        hbm_out=True,
    )
    kv_grad = [sums[0]] + [swap(sums[s], s) for s in range(1, heads)]
    dk, dv = call(
        functools.partial(finish_kv_body, heads),
        [shape(rows, heads * D)] * 2,
        kv_grad,
        scratch=[pltpu.SemaphoreType.DMA((2 * heads,))],
        hbm_out=True,
    )
    return query_grad[None], dk[None], dv[None]


def solution(mesh):
    in_specs = (
        P("ctx", "head", None),
        P("ctx", "head", None),
        P("ctx", "head", None),
        P("ctx", "head", None),
        P("ctx", "head", None),
        P("ctx", None, "head"),
        P(),
    )
    out_specs = (P("ctx", "head", None), P("ctx", "head", None), P("ctx", "head", None))
    return jax.shard_map(steps, mesh=mesh, in_specs=in_specs, out_specs=out_specs, check_vma=False)
```
